32 devices in a mesh: row: 8 (over y, x, core), col: 4 (over z).
Axes of the slice: x: 2, y: 2, z: 4, core: 2. Of those that a mesh axis runs over, the one named last changes fastest.
Arguments:
- trials: float32 [2, 512, 1024], P(None, 'col', 'row'), may hold values from -6 to 6
- valence_factor: float32 [16384, 512], P('row'), may hold values from -0.25 to 0.25
- conduction_factor: float32 [16384, 1024], P('col', 'row'), may hold values from -0.046875 to 0.046875
- screened: float32 [16384, 16384], P('row', 'col'), may hold values from -6 to 6
- valence_energy: float32 [512], P('col'), may hold values from -0.6 to -0.1
- conduction_energy: float32 [1024], P('row'), may hold values from 0.1 to 0.6
Outputs:
- applied: float32 [2, 512, 1024], P(None, 'col', 'row')
The draws below stay inside these ranges and needn't reach their ends.
All inputs are finite; a program needn't handle non-finite values.
Results may differ from the reference program's by a relative error of at most 0.0001.
Values sent between devices are 32-bit elements; how exact they have to be, the bound alone decides.
A program may use at most 256 MiB of HBM per device.

```python
import jax
import jax.numpy as jnp
from jax import lax

V = 512
C = 1024
NP = 16384
B = 2


def steps_of(stream_key, shape, pieces, smallest, largest):
    def one(dim, blocks):
        steps = jax.random.uniform(jax.random.fold_in(jax.random.fold_in(stream_key, 6), dim), (blocks,), jnp.float32, smallest / len(pieces), largest / len(pieces))
        return jnp.repeat(jnp.exp(steps), shape[dim] // blocks).reshape((-1,) + (1,) * (len(shape) - dim - 1))

    loudness = one(*pieces[0])
    for cut in pieces[1:]:
        loudness = loudness * one(*cut)
    return loudness


def normal_values(own_key, shape, spread, bound, pieces=(), dtype=jnp.bfloat16):
    values = jax.random.normal(own_key, shape, jnp.float32) * spread
    if len(pieces) > 0:
        values = steps_of(own_key, shape, pieces, -0.22, 0.18) * values
    return jnp.clip(values, min=-bound, max=bound).astype(dtype)


def setup_inputs(seed: int = 0) -> dict:
    seeds = jax.random.split(jax.random.key(seed), 7)
    return {
        "trials": normal_values(seeds[0], (B, V, C), 1.0, 6.0, ((1, 4), (2, 8)), jnp.float32),
        "valence_factor": normal_values(seeds[1], (NP, V), V ** -0.5, 0.25, ((0, 8),), jnp.float32),
        "conduction_factor": normal_values(seeds[2], (NP, C), NP ** -0.5, 0.046875, ((0, 4), (1, 8)), jnp.float32),
        "screened": normal_values(seeds[3], (NP, NP), 1.0, 6.0, ((0, 8), (1, 4)), jnp.float32),
        "valence_energy": jnp.clip(-0.6 + 0.5 * jax.random.uniform(seeds[4], (V,), jnp.float32) ** steps_of(seeds[4], (V,), ((0, 4),), -0.2, 0.2), -0.6, -0.1),
        "conduction_energy": jnp.clip(0.1 + 0.5 * jax.random.uniform(seeds[5], (C,), jnp.float32) ** steps_of(seeds[5], (C,), ((0, 8),), -0.2, 0.2), 0.1, 0.6),
    }


def reference(trials, valence_factor, conduction_factor, screened, valence_energy, conduction_energy):
    highest = lax.Precision.HIGHEST
    points = jnp.einsum('bvc,nc->bvn', trials, conduction_factor, precision=highest)
    blocks = 16
    block_rows = NP // blocks
    valence_blocks = valence_factor.reshape(blocks, block_rows, V)
    screened_blocks = screened.reshape(blocks, block_rows, NP)

    def accumulate(total, item):
        valence_piece, screened_piece = item
        expanded = jnp.einsum('mv,bvn->bmn', valence_piece, points, precision=highest)
        weighted = expanded * screened_piece[None]
        return total + jnp.einsum('mv,bmn->bvn', valence_piece, weighted, precision=highest), None

    folded, unused = lax.scan(accumulate, jnp.zeros((B, V, NP), jnp.float32), (valence_blocks, screened_blocks))
    kernel_term = jnp.einsum('bvn,nc->bvc', folded, conduction_factor, precision=highest)
    differences = conduction_energy[None, :] - valence_energy[:, None]
    return differences[None] * trials - kernel_term
```

```python
import functools

import jax
import jax.numpy as jnp
from jax import lax
from jax.experimental import pallas as pl
from jax.experimental.pallas import tpu as pltpu
from jax.sharding import PartitionSpec as P

CHUNKS = 4


def split(x):
    high = lax.reduce_precision(x, 8, 7)
    return high.astype(jnp.bfloat16), (x - high).astype(jnp.bfloat16)


def split_in_kernel(x):
    high = x.astype(jnp.bfloat16)
    return high, (x - high.astype(jnp.float32)).astype(jnp.bfloat16)


def dot3(a, b, dims=((1,), (0,))):
    one = lambda x, y: lax.dot_general(x, y, (dims, ((), ())), preferred_element_type=jnp.float32)
    return one(a[0], b[0]) + (one(a[0], b[1]) + one(a[1], b[0]))


def local_kernel(batch, tile_m, first, *refs):
    if first:
        th, tl, vh, vl, wh, wl, factor, screened, out, ph, pw, folded = refs
    else:
        th, tl, vh, vl, wh, wl, factor, screened, before, out, ph, pw, folded = refs
    j, i = pl.program_id(0), pl.program_id(1)
    steps = pl.num_programs(1)
    pieces, tile_n, width = factor.shape
    valence = vh.shape[1]

    @pl.when((j == 0) & (i == 0))
    def _():
        if first:
            out[...] = jnp.zeros_like(out)
        else:
            out[...] = before[...]

    def factor_halves():
        whole = jnp.concatenate([factor[p] for p in range(pieces)], axis=1) if pieces > 1 else factor[0]
        return split_in_kernel(whole)

    @pl.when(i == 0)
    def _():
        halves = factor_halves()
        for b in range(batch):
            rows = pl.ds(b * valence, valence)
            points = dot3((th[rows, :], tl[rows, :]), halves, ((1,), (1,)))
            high, low = split_in_kernel(points)
            ph[:, b * tile_n:(b + 1) * tile_n] = high
            pw[:, b * tile_n:(b + 1) * tile_n] = low
        folded[...] = jnp.zeros_like(folded)

    rows = pl.ds(pl.multiple_of(i * tile_m, tile_m), tile_m)
    left = vh[rows, :], vl[rows, :]
    right = wh[:, rows], wl[:, rows]
    s = screened[...]
    for b in range(batch):
        cols = slice(b * tile_n, (b + 1) * tile_n)
        expanded = dot3(left, (ph[:, cols], pw[:, cols]))
        folded[:, cols] += dot3(right, split_in_kernel(expanded * s))

    @pl.when(i == steps - 1)
    def _():
        halves = factor_halves()
        blocks, part = out.shape[1], out.shape[3]
        for b in range(batch):
            term = dot3(split_in_kernel(folded[:, b * tile_n:(b + 1) * tile_n]), halves)
            for p in range(pieces):
                for q in range(blocks):
                    out[p, q, b] += term[q * part:(q + 1) * part, p * width:(p + 1) * width]


def local_term(start, trials, valence, valence_t, factor, screened, before, batch, blocks):
    pieces, count, width = factor.shape
    rows, depth = valence[0].shape
    tile_m, tile_n = min(512, rows), min(256, count)
    offset = start // tile_n
    first = before is None
    out_shape = (pieces, blocks, batch, depth // blocks, width)
    keep = lambda shape: pl.BlockSpec(shape, lambda j, i: (0,) * len(shape), pipeline_mode=pl.Buffered(1))
    operands = [*trials, *valence, *valence_t, factor, screened]
    in_specs = [keep(x.shape) for x in operands[:6]] + [
        pl.BlockSpec((pieces, tile_n, width), lambda j, i: (0, j, 0)),
        pl.BlockSpec((tile_m, tile_n), lambda j, i: (i, j + offset)),
    ]
    if not first:
        operands.append(before)
        in_specs.append(keep(out_shape))
    flops = 3 * 2 * batch * depth * count * (2 * rows + 2 * pieces * width)
    return pl.pallas_call(
        functools.partial(local_kernel, batch, tile_m, first),
        out_shape=jax.ShapeDtypeStruct(out_shape, jnp.float32),
        grid=(count // tile_n, rows // tile_m),
        in_specs=in_specs,
        out_specs=keep(out_shape),
        scratch_shapes=[
            pltpu.VMEM((depth, batch * tile_n), jnp.bfloat16),
            pltpu.VMEM((depth, batch * tile_n), jnp.bfloat16),
            pltpu.VMEM((depth, batch * tile_n), jnp.float32),
        ],
        compiler_params=pltpu.CompilerParams(vmem_limit_bytes=60 * 1024 * 1024),
        cost_estimate=pl.CostEstimate(flops=flops, bytes_accessed=4 * rows * count, transcendentals=0),
        name="local_term",
    )(*operands)


def body(trials, valence_factor, conduction_factor, screened, valence_energy, conduction_energy):
    row, col = lax.axis_size("row"), lax.axis_size("col")
    batch, part, width = trials.shape
    depth, conduction = part * col, width * row
    every = lax.all_gather(trials, ("col", "row"))
    every = every.reshape(col, row, batch, part, width).transpose(2, 0, 3, 1, 4)
    halves = split(every.reshape(batch * depth, conduction))
    valence, valence_t = split(valence_factor), split(valence_factor.T)
    count = conduction_factor.shape[0] // CHUNKS
    aligned = width % 128 == 0
    total = None
    for k in range(CHUNKS):
        piece = conduction_factor[k * count:(k + 1) * count]
        factor = lax.all_gather(piece, "row") if aligned else lax.all_gather(piece, "row", axis=1, tiled=True)[None]
        total = local_term(k * count, halves, valence, valence_t, factor, screened, total, batch, col)
    if not aligned:
        total = total[0].reshape(col, batch, part, row, width).transpose(3, 0, 1, 2, 4)
    mine = lax.psum_scatter(total, "row")
    kernel_term = lax.psum_scatter(mine, "col")
    differences = conduction_energy[None, :] - valence_energy[:, None]
    return differences[None] * trials - kernel_term


def solution(mesh):
    in_specs = (
        P(None, "col", "row"),
        P("row", None),
        P("col", "row"),
        P("row", "col"),
        P("col"),
        P("row"),
    )
    out_specs = P(None, "col", "row")
    return jax.shard_map(body, mesh=mesh, in_specs=in_specs, out_specs=out_specs, check_vma=False)
```

```python
import functools

import jax
import jax.numpy as jnp
from jax import lax
from jax.experimental import pallas as pl
from jax.experimental.pallas import tpu as pltpu
from jax.sharding import PartitionSpec as P


CHUNKS = 4
TILE_M = 1024
TILE_N = 512
ROWS = 1024


def split(x):
    high = lax.reduce_precision(x, 8, 7)
    return high.astype(jnp.bfloat16), (x - high).astype(jnp.bfloat16)


def split_in_kernel(x):
    high = x.astype(jnp.bfloat16)
    return high, (x - high.astype(jnp.float32)).astype(jnp.bfloat16)


def dot3(a, b, depth_of_b=0):
    left = jnp.concatenate([a[0], a[0], a[1]], axis=1)
    right = jnp.concatenate([b[0], b[1], b[0]], axis=depth_of_b)
    dims = (((1,), (depth_of_b,)), ((), ()))
    return lax.dot_general(left, right, dims, preferred_element_type=jnp.float32)


def local_kernel(limits, first, vh, vl, wh, wl, trials, screened, *refs):
    factors, refs = refs[:len(limits)], refs[len(limits):]
    if not first:
        before, refs = refs[0], refs[1:]
    out, th, tl, ch, cl, ph, pw, folded = refs
    j, i = pl.program_id(0), pl.program_id(1)
    steps = pl.num_programs(1)
    pieces, width = trials.shape[0], trials.shape[2]
    tile_m = screened.shape[0]
    rows = min(ROWS, tile_m)

    def whole(ref):
        return jnp.concatenate([ref[p] for p in range(pieces)], axis=1) if pieces > 1 else ref[0]

    @pl.when((j == 0) & (i == 0))
    def _():
        th[...], tl[...] = split_in_kernel(whole(trials))
        out[...] = jnp.zeros_like(out) if first else before[...]

    for (low, high), factor in zip(limits, factors):

        @pl.when((i == 0) & (j >= low) & (j < high))
        def _():
            ch[...], cl[...] = split_in_kernel(whole(factor))

    @pl.when(i == 0)
    def _():
        points = dot3((th[...], tl[...]), (ch[...], cl[...]), 1)
        ph[...], pw[...] = split_in_kernel(points)

    total = None
    for u in range(tile_m // rows):
        at = pl.ds(pl.multiple_of(i * tile_m + u * rows, rows), rows)
        expanded = dot3((vh[at, :], vl[at, :]), (ph[...], pw[...]))
        weighted = expanded * screened[u * rows:(u + 1) * rows, :]
        term = dot3((wh[:, at], wl[:, at]), split_in_kernel(weighted))
        total = term if total is None else total + term
    folded[...] = jnp.where(i == 0, total, folded[...] + total) if steps > 1 else total

    @pl.when(i == steps - 1)
    def _():
        term = dot3(split_in_kernel(folded[...]), (ch[...], cl[...]))
        blocks, part = out.shape[1], out.shape[2]
        for p in range(pieces):
            for q in range(blocks):
                out[p, q] += term[q * part:(q + 1) * part, p * width:(p + 1) * width]


def local_term(start, valence, valence_t, trials, screened, factors, before, blocks):
    pieces, depth, width = trials.shape
    rows = valence[0].shape[0]
    count = factors[0].shape[1]
    tile_m, tile_n = min(TILE_M, rows), min(TILE_N, count)
    tiles = count // tile_n
    limits = tuple((k * tiles, (k + 1) * tiles) for k in range(len(factors)))
    offset = start // tile_n
    first = before is None
    out_shape = (pieces, blocks, depth // blocks, width)
    keep = lambda shape: pl.BlockSpec(shape, lambda j, i: (0,) * len(shape), pipeline_mode=pl.Buffered(1))
    operands = [*valence, *valence_t, trials, screened, *factors]
    in_specs = [keep(x.shape) for x in operands[:5]]
    in_specs.append(pl.BlockSpec((tile_m, tile_n), lambda j, i: (i, j + offset)))
    for low, high in limits:
        in_specs.append(pl.BlockSpec((pieces, tile_n, width), functools.partial(
            lambda low, high, j, i: (0, jnp.clip(j, low, high - 1) - low, 0), low, high)))
    if not first:
        operands.append(before)
        in_specs.append(keep(out_shape))
    points = count * len(factors)
    conduction = pieces * width
    half = lambda *shape: pltpu.VMEM(shape, jnp.bfloat16)
    return pl.pallas_call(
        functools.partial(local_kernel, limits, first),
        out_shape=jax.ShapeDtypeStruct(out_shape, jnp.float32),
        grid=(tiles * len(factors), rows // tile_m),
        in_specs=in_specs,
        out_specs=keep(out_shape),
        scratch_shapes=[
            half(depth, conduction), half(depth, conduction),
            half(tile_n, conduction), half(tile_n, conduction),
            half(depth, tile_n), half(depth, tile_n),
            pltpu.VMEM((depth, tile_n), jnp.float32),
        ],
        compiler_params=pltpu.CompilerParams(vmem_limit_bytes=60 * 1024 * 1024),
        cost_estimate=pl.CostEstimate(
            flops=12 * depth * points * (rows + conduction), bytes_accessed=4 * rows * points, transcendentals=0),
        name="local_term",
    )(*operands)


def body(trials, valence_factor, conduction_factor, screened, valence_energy, conduction_energy):
    row, col = lax.axis_size("row"), lax.axis_size("col")
    batch, part, width = trials.shape
    count = conduction_factor.shape[0] // CHUNKS
    aligned = width % 128 == 0

    def gather(x):
        return lax.all_gather(x, "row") if aligned else lax.all_gather(x, "row", axis=1, tiled=True)[None]

    factors = [gather(conduction_factor[k * count:(k + 1) * count]) for k in range(CHUNKS)]
    every = lax.all_gather(trials, "col", axis=1, tiled=True)
    vectors = [gather(every[b]) for b in range(batch)]
    valence, valence_t = split(valence_factor), split(valence_factor.T)
    totals = [None] * batch

    def add(b, low, high):
        totals[b] = local_term(
            low * count, valence, valence_t, vectors[b], screened, factors[low:high], totals[b], col)

    def owned(b):
        total = totals[b]
        if not aligned:
            total = total[0].reshape(col, part, row, width).transpose(2, 0, 1, 3)
        return lax.psum_scatter(total, "row")

    half = CHUNKS // 2
    for b in range(batch):
        if b == 0:
            for k in range(half):
                add(b, k, k + 1)
        else:
            add(b, 0, half)
    totals = list(lax.optimization_barrier(tuple(totals)))
    terms = []
    for b in range(batch):
        if b == 0:
            for k in range(half, CHUNKS):
                add(b, k, k + 1)
        else:
            add(b, half, CHUNKS)
        terms.append(owned(b))
    swapped = lax.all_to_all(jnp.stack(terms, axis=1), "col", split_axis=0, concat_axis=0, tiled=True)
    kernel_term = swapped.sum(axis=0)
    differences = conduction_energy[None, :] - valence_energy[:, None]
    return differences[None] * trials - kernel_term


def solution(mesh):
    in_specs = (
        P(None, "col", "row"),
        P("row", None),
        P("col", "row"),
        P("row", "col"),
        P("col"),
        P("row"),
    )
    out_specs = P(None, "col", "row")
    return jax.shard_map(body, mesh=mesh, in_specs=in_specs, out_specs=out_specs, check_vma=False)
```

```python
import functools

import jax
import jax.numpy as jnp
from jax import lax
from jax.experimental import pallas as pl
from jax.experimental.pallas import tpu as pltpu
from jax.sharding import PartitionSpec as P


CHUNKS = 4
TILE_M = 1024
TILE_N = 512
ROWS = 1024


def split(x):
    high = lax.reduce_precision(x, 8, 7)
    return high.astype(jnp.bfloat16), (x - high).astype(jnp.bfloat16)


def split_in_kernel(x):
    high = x.astype(jnp.bfloat16)
    return high, (x - high.astype(jnp.float32)).astype(jnp.bfloat16)


def dot3(a, b, depth_of_b=0):
    left = jnp.concatenate([a[0], a[0], a[1]], axis=1)
    right = jnp.concatenate([b[0], b[1], b[0]], axis=depth_of_b)
    dims = (((1,), (depth_of_b,)), ((), ()))
    return lax.dot_general(left, right, dims, preferred_element_type=jnp.float32)


def local_kernel(limits, first, vh, vl, wh, wl, trials, screened, *refs):
    factors, refs = refs[:len(limits)], refs[len(limits):]
    if not first:
        before, refs = refs[0], refs[1:]
    out, th, tl, ch, cl, ph, pw, folded = refs
    j, i = pl.program_id(0), pl.program_id(1)
    steps = pl.num_programs(1)
    pieces, width = trials.shape[0], trials.shape[2]
    tile_m = screened.shape[0]
    rows = min(ROWS, tile_m)

    def whole(ref):
        return jnp.concatenate([ref[p] for p in range(pieces)], axis=1) if pieces > 1 else ref[0]

    @pl.when((j == 0) & (i == 0))
    def _():
        th[...], tl[...] = split_in_kernel(whole(trials))
        out[...] = jnp.zeros_like(out) if first else before[...]

    for (low, high), factor in zip(limits, factors):

        @pl.when((i == 0) & (j >= low) & (j < high))
        def _():
            ch[...], cl[...] = split_in_kernel(whole(factor))

    @pl.when(i == 0)
    def _():
        points = dot3((th[...], tl[...]), (ch[...], cl[...]), 1)
        ph[...], pw[...] = split_in_kernel(points)

    total = None
    for u in range(tile_m // rows):
        at = pl.ds(pl.multiple_of(i * tile_m + u * rows, rows), rows)
        expanded = dot3((vh[at, :], vl[at, :]), (ph[...], pw[...]))
        weighted = expanded * screened[u * rows:(u + 1) * rows, :]
        term = dot3((wh[:, at], wl[:, at]), split_in_kernel(weighted))
        total = term if total is None else total + term
    folded[...] = jnp.where(i == 0, total, folded[...] + total) if steps > 1 else total

    @pl.when(i == steps - 1)
    def _():
        term = dot3(split_in_kernel(folded[...]), (ch[...], cl[...]))
        blocks, part = out.shape[1], out.shape[2]
        for p in range(pieces):
            for q in range(blocks):
                out[p, q] += term[q * part:(q + 1) * part, p * width:(p + 1) * width]


def local_term(start, valence, valence_t, trials, screened, factors, before, blocks):
    pieces, depth, width = trials.shape
    rows = valence[0].shape[0]
    count = factors[0].shape[1]
    tile_m, tile_n = min(TILE_M, rows), min(TILE_N, count)
    tiles = count // tile_n
    limits = tuple((k * tiles, (k + 1) * tiles) for k in range(len(factors)))
    offset = start // tile_n
    first = before is None
    out_shape = (pieces, blocks, depth // blocks, width)
    keep = lambda shape: pl.BlockSpec(shape, lambda j, i: (0,) * len(shape), pipeline_mode=pl.Buffered(1))
    operands = [*valence, *valence_t, trials, screened, *factors]
    in_specs = [keep(x.shape) for x in operands[:5]]
    in_specs.append(pl.BlockSpec((tile_m, tile_n), lambda j, i: (i, j + offset)))
    for low, high in limits:
        in_specs.append(pl.BlockSpec((pieces, tile_n, width), functools.partial(
            lambda low, high, j, i: (0, jnp.clip(j, low, high - 1) - low, 0), low, high)))
    if not first:
        operands.append(before)
        in_specs.append(keep(out_shape))
    points = count * len(factors)
    conduction = pieces * width
    half = lambda *shape: pltpu.VMEM(shape, jnp.bfloat16)
    return pl.pallas_call(
        functools.partial(local_kernel, limits, first),
        out_shape=jax.ShapeDtypeStruct(out_shape, jnp.float32),
        grid=(tiles * len(factors), rows // tile_m),
        in_specs=in_specs,
        out_specs=keep(out_shape),
        scratch_shapes=[
            half(depth, conduction), half(depth, conduction),
            half(tile_n, conduction), half(tile_n, conduction),
            half(depth, tile_n), half(depth, tile_n),
            pltpu.VMEM((depth, tile_n), jnp.float32),
        ],
        compiler_params=pltpu.CompilerParams(vmem_limit_bytes=60 * 1024 * 1024),
        cost_estimate=pl.CostEstimate(
            flops=12 * depth * points * (rows + conduction), bytes_accessed=4 * rows * points, transcendentals=0),
        name="local_term",
    )(*operands)


def body(trials, valence_factor, conduction_factor, screened, valence_energy, conduction_energy):
    row, col = lax.axis_size("row"), lax.axis_size("col")
    batch, part, width = trials.shape
    count = conduction_factor.shape[0] // CHUNKS
    aligned = width % 128 == 0

    def gather(x):
        return lax.all_gather(x, "row") if aligned else lax.all_gather(x, "row", axis=1, tiled=True)[None]

    factors = [gather(conduction_factor[k * count:(k + 1) * count]) for k in range(CHUNKS)]
    every = lax.all_gather(trials, "col", axis=1, tiled=True)
    copies = jnp.broadcast_to(every[0], (row,) + every[0].shape)
    first = lax.all_to_all(copies, "row", split_axis=0, concat_axis=0, tiled=True)
    if not aligned:
        first = first.transpose(1, 0, 2).reshape(1, part * col, row * width)
    vectors = [first] + [gather(every[b]) for b in range(1, batch)]
    valence, valence_t = split(valence_factor), split(valence_factor.T)
    totals = [None] * batch

    def add(b, low, high):
        totals[b] = local_term(
            low * count, valence, valence_t, vectors[b], screened, factors[low:high], totals[b], col)

    def owned(b):
        total = totals[b]
        if not aligned:
            total = total[0].reshape(col, part, row, width).transpose(2, 0, 1, 3)
        if b < batch - 1:
            return lax.psum_scatter(total, "row")
        return lax.all_to_all(total, "row", split_axis=0, concat_axis=0, tiled=True).sum(axis=0)

    half = CHUNKS // 2
    for b in range(batch):
        if b == 0:
            for k in range(half):
                add(b, k, k + 1)
        else:
            add(b, 0, half)
    totals = list(lax.optimization_barrier(tuple(totals)))
    terms = []
    for b in range(batch):
        if b == 0:
            for k in range(half, CHUNKS):
                add(b, k, k + 1)
        else:
            add(b, half, CHUNKS)
        terms.append(owned(b))
    swapped = lax.all_to_all(jnp.stack(terms, axis=1), "col", split_axis=0, concat_axis=0, tiled=True)
    kernel_term = swapped.sum(axis=0)
    differences = conduction_energy[None, :] - valence_energy[:, None]
    return differences[None] * trials - kernel_term


def solution(mesh):
    in_specs = (
        P(None, "col", "row"),
        P("row", None),
        P("col", "row"),
        P("row", "col"),
        P("col"),
        P("row"),
    )
    out_specs = P(None, "col", "row")
    return jax.shard_map(body, mesh=mesh, in_specs=in_specs, out_specs=out_specs, check_vma=False)
```
